32 devices in a mesh: grp: 4 (over y, core), tbl: 8 (over z, x).
Axes of the slice: x: 2, y: 2, z: 4, core: 2. Of those that a mesh axis runs over, the one named last changes fastest.
Arguments:
- user_feats: bfloat16 [512, 128], P(('grp', 'tbl')), may hold values from -6 to 6
- tower_in: bfloat16 [128, 4096], replicated, may hold values from -0.5 to 0.5
- tower_out: bfloat16 [4096, 256], replicated, may hold values from -0.09375 to 0.09375
- table: bfloat16 [2048, 256], P('tbl'), may hold values from -3 to 3
- inter_weight: bfloat16 [256, 512], replicated, may hold values from -0.375 to 0.375
- out_weight: float32 [512], replicated, may hold values from -0.3 to 0.3
- ids: int32 [32, 8, 4, 32], P(('grp', 'tbl')), may hold values from 0 to 255
- live: int32 [32, 8], P(('grp', 'tbl')), may hold values from 1 to 32, as said below
- req_of: int32 [32, 8, 32], P(('grp', 'tbl')), may hold values from 0 to 127
- labels: float32 [32, 8, 32], P(('grp', 'tbl')), may hold values from 0 to 1
Outputs:
- scores: float32 [32, 8, 32], P(('grp', 'tbl'))
- grad_tower_in: float32 [128, 4096], replicated
- grad_tower_out: float32 [4096, 256], replicated
- grad_inter: float32 [256, 512], replicated
- grad_out: float32 [512], replicated
- grad_table: float32 [2048, 256], P('tbl')
The draws below stay inside these ranges and needn't reach their ends.
Inputs may be any that keep to these rules, and one draw needn't show every extreme that they name: In every draw, in each group, some device gets 32 live slots from every owner; the others get between 1 and 32 live slots from each owner.
All inputs are finite; a program needn't handle non-finite values.
Results may differ from the reference program's by a relative error of at most 0.0067.
Values may be sent and summed in bfloat16 or wider, within the bound.
A program may use at most 64 MiB of HBM per device.

```python
import math
import jax
import jax.numpy as jnp
import numpy as np
from jax import lax

UF = 128
H = 4096
E = 256
HI = 512
BAG = 4
SLOT = 32
TROWS_DEV = 256
REQ_GRP = 128
N_GRP = 4
N_TBL = 8


def draw_live(key, part):
    base_key = jax.random.fold_in(key, 11)
    first, second, third = jax.random.split(base_key, 3)
    factor = jax.random.randint(first, (N_GRP, 1, N_TBL), 1, 5)
    base = jax.random.randint(second, (N_GRP, N_TBL, N_TBL), 0, SLOT)
    counts = 1 + base * factor // 4
    full = jax.random.randint(third, (N_GRP, 1, 1), 0, N_TBL)
    dest = jnp.arange(N_TBL, dtype=jnp.int32)[None, :, None]
    counts = jnp.where(dest == full, SLOT, counts)
    return counts.reshape(N_GRP * N_TBL, N_TBL).astype(jnp.int32)


def touch_ends(drawn, own_key, least, largest):
    place = [jax.random.randint(jax.random.fold_in(own_key, axis), (), 0, length) for axis, length in enumerate(drawn.shape)]
    longest = drawn.shape.index(max(drawn.shape))
    next_to = place[:longest] + [(place[longest] + 1) % drawn.shape[longest]] + place[longest + 1:]
    return drawn.at[tuple(place)].set(least).at[tuple(next_to)].set(largest)


def block_scale(rng, dims, pieces, least, top_value):
    def one(position, parts):
        steps = jax.random.uniform(jax.random.fold_in(jax.random.fold_in(rng, 6), position), (parts,), jnp.float32, least / len(pieces), top_value / len(pieces))
        return jnp.repeat(jnp.exp(steps), dims[position] // parts).reshape((-1,) + (1,) * (len(dims) - position - 1))

    level = one(*pieces[0])
    for cut in pieces[1:]:
        level = level * one(*cut)
    return level


def rank_bounds(count, lean):
    weights = [(1 << 20) // math.isqrt(rank ** lean) + 1 for rank in range(1, count + 1)]
    scale = 1 + sum(weights) // (1 << 30)
    return np.cumsum(np.array([max(1, weight // scale) for weight in weights]))


def ranked_ids(stream_key, extent, number_of, slope):
    grid = rank_bounds(number_of, slope)
    lot = jax.random.randint(jax.random.fold_in(stream_key, 1), extent, 0, int(grid[number_of - 1]))
    standing = jnp.searchsorted(jnp.asarray(grid, jnp.int32), lot, side="right")
    return jax.random.permutation(jax.random.fold_in(stream_key, 2), number_of)[standing].astype(jnp.int32)


def noise(stream_key, dims, scale, limit, shards=(), held_as=jnp.bfloat16):
    entries = scale * jax.random.normal(stream_key, dims, jnp.float32)
    if shards:
        entries = entries * block_scale(stream_key, dims, shards, -0.22, 0.18)
    return jnp.clip(entries, -limit, limit).astype(held_as)


def setup_inputs(seed: int = 0) -> dict:
    key_of = jax.random.split(jax.random.key(seed), 11)
    user_feats = noise(key_of[0], (N_GRP * REQ_GRP, UF), 1.0, 6.0, ((0, 32),))
    tower_in = noise(key_of[1], (UF, H), UF ** -0.5, 0.5)
    tower_out = noise(key_of[2], (H, E), H ** -0.5, 0.09375)
    table = noise(key_of[3], (N_TBL * TROWS_DEV, E), 0.5, 3.0, ((0, 8),))
    inter_weight = noise(key_of[4], (E, HI), E ** -0.5, 0.375)
    out_weight = noise(key_of[5], (HI,), 0.05, 0.3, (), jnp.float32)
    ids = touch_ends(jax.random.randint(key_of[6], (N_GRP * N_TBL, N_TBL, BAG, SLOT), 0, TROWS_DEV), jax.random.fold_in(key_of[6], 1), 0, TROWS_DEV - 1).astype(jnp.int32)
    live = draw_live(jax.random.fold_in(key_of[10], 71), 0)
    req_of = touch_ends(ranked_ids(key_of[8], (N_GRP * N_TBL, N_TBL, SLOT), REQ_GRP, 2), jax.random.fold_in(key_of[8], 3), 0, REQ_GRP - 1).astype(jnp.int32)
    labels = jnp.clip(1.0 * jax.random.uniform(key_of[9], (N_GRP * N_TBL, N_TBL, SLOT), jnp.float32) ** block_scale(key_of[9], (N_GRP * N_TBL, N_TBL, SLOT), ((0, 32),), -0.2, 0.2), 0.0, 1.0)
    return dict(user_feats=user_feats, tower_in=tower_in, tower_out=tower_out, table=table, inter_weight=inter_weight, out_weight=out_weight, ids=ids, live=live, req_of=req_of, labels=labels)


def silu_slope(value):
    sig = jax.nn.sigmoid(value)
    return sig * (1.0 + value * (1.0 - sig))

def reference(user_feats, tower_in, tower_out, table, inter_weight, out_weight, ids, live, req_of, labels):
    highest = lax.Precision.HIGHEST
    pre = jnp.dot(user_feats, tower_in, preferred_element_type=jnp.float32)
    hidden = jax.nn.silu(pre).astype(jnp.bfloat16)
    users = jnp.dot(hidden, tower_out, preferred_element_type=jnp.float32).astype(jnp.bfloat16)
    factor = 1.0 / math.sqrt(N_GRP * N_TBL * N_TBL * SLOT)
    offset = (jnp.arange(N_TBL, dtype=jnp.int32) * TROWS_DEV)[:, None, None]
    slot_index = jnp.arange(SLOT, dtype=jnp.int32)
    grad_inter = jnp.zeros((E, HI), jnp.float32)
    grad_out = jnp.zeros((HI,), jnp.float32)
    grad_table = jnp.zeros((N_TBL * TROWS_DEV, E), jnp.float32)
    score_list = []
    duser_list = []
    for group in range(N_GRP):
        lo = group * N_TBL
        group_ids = ids[lo:lo + N_TBL]
        summed = jnp.zeros((N_TBL, N_TBL, SLOT, E), jnp.float32)
        for bag in range(BAG):
            summed = summed + table[group_ids[:, :, bag, :] + offset].astype(jnp.float32)
        pooled = summed.astype(jnp.bfloat16)
        items = jnp.transpose(pooled, (1, 0, 2, 3)).reshape(-1, E)
        request = req_of[lo:lo + N_TBL].reshape(-1).astype(jnp.int32)
        group_users = users[group * REQ_GRP:(group + 1) * REQ_GRP]
        chosen = group_users[request]
        cross = (items.astype(jnp.float32) * chosen.astype(jnp.float32)).astype(jnp.bfloat16)
        inner = jnp.dot(cross, inter_weight, preferred_element_type=jnp.float32)
        act = jax.nn.silu(inner)
        score = lax.optimization_barrier(jnp.sum(act * out_weight, axis=1))
        mask = (slot_index[None, None, :] < live[lo:lo + N_TBL][:, :, None]).reshape(-1)
        target = labels[lo:lo + N_TBL].reshape(-1)
        grad_score = jnp.where(mask, jax.nn.sigmoid(score) - target, 0.0) * factor
        dinner = (grad_score[:, None] * out_weight * silu_slope(inner)).astype(jnp.bfloat16)
        grad_inter = grad_inter + jnp.dot(cross.T, dinner, preferred_element_type=jnp.float32)
        grad_out = grad_out + lax.optimization_barrier(jnp.sum(grad_score[:, None] * act, axis=0))
        dcross = jnp.dot(dinner, inter_weight.T, preferred_element_type=jnp.float32)
        d_item = dcross * chosen.astype(jnp.float32)
        d_user = dcross * items.astype(jnp.float32)
        duser_list.append(jax.ops.segment_sum(d_user, request, num_segments=REQ_GRP))
        back = jnp.transpose(d_item.reshape(N_TBL, N_TBL, SLOT, E), (1, 0, 2, 3)).reshape(-1, E)
        for bag in range(BAG):
            where_rows = (group_ids[:, :, bag, :] + offset).reshape(-1).astype(jnp.int32)
            grad_table = grad_table + jax.ops.segment_sum(back, where_rows, num_segments=N_TBL * TROWS_DEV)
        score_list.append(score.reshape(N_TBL, N_TBL, SLOT))
    d_users = jnp.concatenate(duser_list, axis=0)
    grad_tower_out = jnp.dot(hidden.astype(jnp.float32).T, d_users, precision=highest)
    d_hidden = jnp.dot(d_users, tower_out.astype(jnp.float32).T, precision=highest)
    d_pre = d_hidden * silu_slope(pre)
    grad_tower_in = jnp.dot(user_feats.astype(jnp.float32).T, d_pre, precision=highest)
    scores = jnp.concatenate(score_list, axis=0)
    return (scores, grad_tower_in, grad_tower_out, grad_inter, grad_out, grad_table)
```

```python
import functools
import math

import jax
import jax.numpy as jnp
from jax import lax
from jax.experimental import pallas as pl
from jax.experimental.pallas import tpu as pltpu
from jax.sharding import PartitionSpec as P

BF = jnp.bfloat16
F32 = jnp.float32
MESH = pl.DeviceIdType.MESH


def silu_slope(value):
    sig = jax.nn.sigmoid(value)
    return sig * (1.0 + value * (1.0 - sig))


def exchange_kernel(groups, shards, plan, *refs):
    count = len(plan)
    ins = refs[:count]
    outs = refs[count : 2 * count]
    send_sem, recv_sem, own_sem = refs[2 * count :]
    total = groups * shards
    my_grp = lax.axis_index("grp")
    my_tbl = lax.axis_index("tbl")
    me = my_grp * shards + my_tbl

    def size_of(scope):
        return {"all": total, "tbl": shards, "grp": groups}[scope]

    def place_of(scope):
        return {"all": me, "tbl": my_tbl, "grp": my_grp}[scope]

    def source(n, where):
        return ins[n].at[where] if plan[n][1] == "scatter" else ins[n]

    barrier = pltpu.get_barrier_semaphore()

    def greet(step, carry):
        peer = lax.rem(me + step, total)
        pl.semaphore_signal(
            barrier, inc=1, device_id=(peer // shards, peer % shards), device_id_type=MESH
        )
        return carry

    lax.fori_loop(1, total, greet, 0)
    for n, (scope, kind) in enumerate(plan):
        here = place_of(scope)
        pltpu.make_async_copy(source(n, here), outs[n].at[here], own_sem.at[n]).start()
    pl.semaphore_wait(barrier, total - 1)

    for wanted in ("tbl", "grp", "all"):
        chosen = [n for n in range(count) if plan[n][0] == wanted]
        if not chosen:
            continue
        size = size_of(wanted)
        here = place_of(wanted)

        def push(step, carry):
            there = lax.rem(here + step, size)
            if wanted == "all":
                target = (there // shards, there % shards)
            elif wanted == "tbl":
                target = (my_grp, there)
            else:
                target = (there, my_tbl)
            for n in chosen:
                pltpu.make_async_remote_copy(
                    src_ref=source(n, there),
                    dst_ref=outs[n].at[here],
                    send_sem=send_sem.at[n],
                    recv_sem=recv_sem.at[n],
                    device_id=target,
                    device_id_type=MESH,
                ).start()
            return carry

        lax.fori_loop(1, size, push, 0)
    for n, (scope, kind) in enumerate(plan):
        here = place_of(scope)
        others = outs[n].at[pl.ds(0, size_of(scope) - 1)]
        pltpu.make_async_copy(source(n, here), outs[n].at[here], own_sem.at[n]).wait()
        pltpu.make_async_copy(others, others, send_sem.at[n]).wait()
        pltpu.make_async_copy(others, others, recv_sem.at[n]).wait()


def exchange(ident, groups, shards, *items):
    plan = tuple((scope, kind) for scope, kind, _ in items)
    arrays = [array for _, _, array in items]
    sizes = {"all": groups * shards, "tbl": shards, "grp": groups}
    shapes = []
    for scope, kind, array in items:
        block = array.shape[1:] if kind == "scatter" else array.shape
        shapes.append(jax.ShapeDtypeStruct((sizes[scope],) + block, array.dtype))
    vmem = pl.BlockSpec(memory_space=pltpu.VMEM)
    return pl.pallas_call(
        functools.partial(exchange_kernel, groups, shards, plan),
        out_shape=shapes,
        in_specs=[vmem] * len(arrays),
        out_specs=[vmem] * len(arrays),
        scratch_shapes=[pltpu.SemaphoreType.DMA((len(arrays),))] * 3,
        compiler_params=pltpu.CompilerParams(collective_id=ident, has_side_effects=True),
        name="exchange_%d" % ident,
    )(*arrays)


def dot(a, b, ca, cb):
    return lax.dot_general(a, b, (((ca,), (cb,)), ((), ())), preferred_element_type=F32)


def body(
    user_feats, tower_in, tower_out, table, inter_weight, out_weight, ids, live, req_of, labels
):
    groups = lax.axis_size("grp")
    shards = lax.axis_size("tbl")
    total = groups * shards
    rows_table, width = table.shape
    slots = ids.shape[3]
    cands = shards * slots
    rows_user, feats = user_feats.shape
    group_rows = rows_user * shards
    units = inter_weight.shape[1]

    bags = jnp.swapaxes(ids[0], 1, 2).reshape(cands, -1)
    counts = jnp.sum(
        (bags[:, :, None] == jnp.arange(rows_table, dtype=jnp.int32)).astype(F32), axis=1
    ).astype(BF)
    pooled = dot(counts, table, 1, 0).astype(BF)
    items, all_feats = exchange(
        0,
        groups,
        shards,
        ("tbl", "scatter", pooled.reshape(shards, slots, width)),
        ("all", "gather", user_feats),
    )
    items = items.reshape(cands, width)
    all_feats = all_feats.reshape(total * rows_user, feats)
    group_feats = lax.dynamic_slice_in_dim(
        all_feats, lax.axis_index("grp") * group_rows, group_rows, 0
    )
    group_hidden = jax.nn.silu(dot(group_feats, tower_in, 1, 0)).astype(BF)
    users = dot(group_hidden, tower_out, 1, 0).astype(BF)
    request = req_of[0].reshape(-1)
    picks = (request[:, None] == jnp.arange(group_rows, dtype=jnp.int32)).astype(BF)
    chosen = dot(picks, users, 1, 0)
    items32 = items.astype(F32)
    cross = (items32 * chosen).astype(BF)
    inner = dot(cross, inter_weight, 1, 0)
    act = jax.nn.silu(inner)
    score = jnp.sum(act * out_weight, axis=1)
    factor = 1.0 / math.sqrt(groups * shards * shards * slots)
    slot_index = jnp.arange(slots, dtype=jnp.int32)
    mask = (slot_index[None, :] < live[0][:, None]).reshape(-1)
    target = labels[0].reshape(-1)
    grad_score = jnp.where(mask, jax.nn.sigmoid(score) - target, 0.0) * factor
    dinner = (grad_score[:, None] * out_weight * silu_slope(inner)).astype(BF)
    grad_inter = dot(cross, dinner, 0, 0).astype(BF)
    grad_out = jnp.sum(grad_score[:, None] * act, axis=0)
    dcross = dot(dinner, inter_weight, 1, 1)
    d_item = (dcross * chosen).astype(BF)
    d_user = (dcross * items32).astype(BF)
    user_terms = dot(picks, d_user, 0, 0).astype(BF)

    back, user_parts, inter_parts, out_parts = exchange(
        1,
        groups,
        shards,
        ("tbl", "scatter", d_item.reshape(shards, slots, width)),
        ("tbl", "scatter", user_terms.reshape(shards, rows_user, width)),
        ("all", "scatter", grad_inter.reshape(total, width // total, units)),
        ("all", "gather", grad_out.reshape(-1, 128)),
    )
    d_users_own = jnp.sum(user_parts.astype(F32), axis=0).astype(BF)
    inter_own = jnp.sum(inter_parts.astype(F32), axis=0).astype(BF)
    grad_out_total = jnp.sum(out_parts, axis=0).reshape(units)
    table_local = dot(counts, back.reshape(cands, width), 0, 0).astype(BF)

    table_parts, d_users, inter_all = exchange(
        2,
        groups,
        shards,
        ("grp", "gather", table_local),
        ("all", "gather", d_users_own),
        ("all", "gather", inter_own),
    )
    grad_table = jnp.sum(table_parts.astype(F32), axis=0)
    grad_inter_total = inter_all.reshape(width, units).astype(F32)
    d_users = d_users.reshape(total * rows_user, width)

    def tower_grads(part_feats, part_users):
        pre = dot(part_feats, tower_in, 1, 0)
        hidden = jax.nn.silu(pre).astype(BF)
        grad_out_part = dot(hidden, part_users, 0, 0)
        d_pre = (dot(part_users, tower_out, 1, 1) * silu_slope(pre)).astype(BF)
        return dot(part_feats, d_pre, 0, 0), grad_out_part

    rows_all = total * rows_user
    chunk = math.gcd(rows_all, 512)
    if chunk == rows_all:
        grad_tower_in, grad_tower_out = tower_grads(all_feats, d_users)
    else:

        def step(index, sums):
            one, two = tower_grads(
                lax.dynamic_slice_in_dim(all_feats, index * chunk, chunk, 0),
                lax.dynamic_slice_in_dim(d_users, index * chunk, chunk, 0),
            )
            return sums[0] + one, sums[1] + two

        grad_tower_in, grad_tower_out = lax.fori_loop(
            0,
            rows_all // chunk,
            step,
            (jnp.zeros(tower_in.shape, F32), jnp.zeros(tower_out.shape, F32)),
        )
    scores = score.reshape(1, shards, slots)
    return (scores, grad_tower_in, grad_tower_out, grad_inter_total, grad_out_total, grad_table)


def solution(mesh):
    placed = (
        P(("grp", "tbl"), None),
        P(),
        P(),
        P("tbl", None),
        P(),
        P(),
        P(("grp", "tbl"), None, None, None),
        P(("grp", "tbl"), None),
        P(("grp", "tbl"), None, None),
        P(("grp", "tbl"), None, None),
    )
    return jax.shard_map(
        body,
        mesh=mesh,
        in_specs=placed,
        out_specs=(P(("grp", "tbl"), None, None), P(), P(), P(), P(), P("tbl", None)),
        check_vma=False,
    )
```

```python
import functools
import math

import jax
import jax.numpy as jnp
from jax import lax
from jax.experimental import pallas as pl
from jax.experimental.pallas import tpu as pltpu
from jax.sharding import PartitionSpec as P

BF = jnp.bfloat16
F32 = jnp.float32
MESH = pl.DeviceIdType.MESH


def silu_slope(value):
    sig = jax.nn.sigmoid(value)
    return sig * (1.0 + value * (1.0 - sig))


def dot(a, b, ca, cb):
    return lax.dot_general(a, b, (((ca,), (cb,)), ((), ())), preferred_element_type=F32)


def step_kernel(groups, shards, slots, bags, tile, in_place, *refs):
    refs = list(refs)
    take = lambda n: [refs.pop(0) for _ in range(n)]
    feats, t_in, t_out, table, weight, out_w, cols, rows = take(8)
    scores, g_inter, g_out, g_table, tower_a, tower_b = take(6)
    pool_s, pool_r, feat_r, item_s, item_r, term_s, term_r = take(7)
    inter_s, inter_r, out_s, out_r, mine_s, users_r, part_s, part_r, sum_s, sum_r = take(10)
    if in_place:
        t_in_t, hidden_t, slope_t = take(3)
    send_sem, recv_sem, own_sem = take(3)
    total = groups * shards
    my_grp = lax.axis_index("grp")
    my_tbl = lax.axis_index("tbl")
    me = my_grp * shards + my_tbl
    rows_table, width = table.shape
    hidden_width = t_out.shape[0]
    units = weight.shape[1]
    cands = cols.shape[0]
    rows_user = feats.shape[0]
    group_rows = shards * rows_user
    sizes = {"all": total, "tbl": shards, "grp": groups, "far": total - shards + 1}
    places = {"all": me, "tbl": my_tbl, "grp": my_grp}
    links = {
        "pool": (0, "tbl", pool_s, pool_r, True),
        "near": (1, "tbl", feats, feat_r, False),
        "far": (2, "far", feats, feat_r, False),
        "item": (3, "tbl", item_s, item_r, True),
        "term": (4, "tbl", term_s, term_r, True),
        "inter": (5, "all", inter_s, inter_r, True),
        "out": (6, "all", out_s, out_r, False),
        "mine": (7, "all", mine_s, users_r, False),
        "part": (8, "grp", part_s, part_r, False),
        "sum": (9, "all", sum_s, sum_r, False),
    }

    def spot(name):
        return me if name in ("near", "far") else places[links[name][1]]

    def origin(name, where):
        _, _, source, _, scatter = links[name]
        return source.at[where] if scatter else source

    def own(name):
        sem, _, _, target, _ = links[name]
        here = spot(name)
        return pltpu.make_async_copy(origin(name, here), target.at[here], own_sem.at[sem])

    def push(*names):
        scope = links[names[0]][1]
        for name in names:
            if name != "far":
                own(name).start()

        def one(step, carry):
            if scope == "all":
                there = lax.rem(me + step, total)
                device = (there // shards, there % shards)
            elif scope == "tbl":
                there = lax.rem(my_tbl + step, shards)
                device = (my_grp, there)
            elif scope == "grp":
                there = lax.rem(my_grp + step, groups)
                device = (there, my_tbl)
            else:
                there = lax.rem((my_grp + 1) * shards + step - 1, total)
                device = (there // shards, there % shards)
            for name in names:
                sem, _, _, target, _ = links[name]
                pltpu.make_async_remote_copy(
                    src_ref=origin(name, there),
                    dst_ref=target.at[spot(name)],
                    send_sem=send_sem.at[sem],
                    recv_sem=recv_sem.at[sem],
                    device_id=device,
                    device_id_type=MESH,
                ).start()
            return carry

        lax.fori_loop(1, sizes[scope], one, 0)

    def others(name):
        _, scope, _, target, _ = links[name]
        return target.at[pl.ds(0, sizes[scope] - 1)]

    def arrive(name):
        if name != "far":
            own(name).wait()
        pltpu.make_async_copy(others(name), others(name), recv_sem.at[links[name][0]]).wait()

    barrier = pltpu.get_barrier_semaphore()

    def greet(step, carry):
        peer = lax.rem(me + step, total)
        pl.semaphore_signal(
            barrier, inc=1, device_id=(peer // shards, peer % shards), device_id_type=MESH
        )
        return carry

    lax.fori_loop(1, total, greet, 0)

    lane = lax.broadcasted_iota(jnp.int32, (cands, rows_table), 1).astype(F32)
    counts = jnp.zeros((cands, rows_table), F32)
    for bag in range(bags):
        counts = counts + jnp.where(cols[:, bag : bag + 1] == lane, 1.0, 0.0)
    pooled = dot(counts.astype(BF), table[...], 1, 0)
    pool_s[...] = pooled.reshape(shards, slots, width).astype(BF)
    pl.semaphore_wait(barrier, total - 1)
    push("near", "pool")
    push("far")
    if in_place:

        def flip(index, carry):
            at = pl.ds(pl.multiple_of(index * tile, tile), tile)
            t_in_t[at, :] = t_in[:, at].T
            return carry

        lax.fori_loop(0, hidden_width // tile, flip, 0)

    arrive("near")
    group_feats = feat_r[pl.ds(my_grp * shards, shards)].reshape(group_rows, -1)

    def forward(index, acc):
        at = pl.ds(pl.multiple_of(index * tile, tile), tile)
        pre = dot(group_feats, t_in[:, at], 1, 0)
        hidden = (pre * jax.nn.sigmoid(pre)).astype(BF)
        return acc + dot(hidden, t_out[at, :], 1, 0)

    users = lax.fori_loop(
        0, hidden_width // tile, forward, jnp.zeros((group_rows, width), F32)
    ).astype(BF)
    lane = lax.broadcasted_iota(jnp.int32, (cands, group_rows), 1).astype(F32)
    picks = jnp.where(cols[:, bags : bags + 1] == lane, 1.0, 0.0).astype(BF)
    chosen = dot(picks, users, 1, 0)
    arrive("pool")
    items = pool_r[...].reshape(cands, width).astype(F32)
    cross = (items * chosen).astype(BF)
    inner = dot(cross, weight[...], 1, 0)
    sig = jax.nn.sigmoid(inner)
    act = inner * sig
    score = jnp.sum(act * out_w[...], axis=1, keepdims=True)
    scores[...] = score
    factor = 1.0 / math.sqrt(groups * shards * shards * slots)
    grad = cols[:, bags + 1 : bags + 2] * (jax.nn.sigmoid(score) - cols[:, bags + 2 : bags + 3]) * factor
    slope = sig * (1.0 + inner * (1.0 - sig))
    dinner = (grad * out_w[...] * slope).astype(BF)
    dcross = dot(dinner, weight[...], 1, 1)
    item_s[...] = (dcross * chosen).reshape(shards, slots, width).astype(BF)
    side = lax.broadcasted_iota(jnp.int32, (group_rows, cands), 0).astype(F32)
    picks_t = jnp.where(rows[bags : bags + 1, :] == side, 1.0, 0.0).astype(BF)
    terms = dot(picks_t, (dcross * items).astype(BF), 1, 0)
    term_s[...] = terms.reshape(shards, rows_user, width).astype(BF)
    push("term", "item")
    out_s[...] = jnp.sum(grad * act, axis=0, keepdims=True)
    inter = dot(cross, dinner, 0, 0)
    inter_s[...] = inter.reshape(total, width // total, units).astype(BF)
    push("inter", "out")
    arrive("far")
    all_rows = total * rows_user
    if in_place:
        all_feats = feat_r[...].reshape(all_rows, -1)

        def ahead(index, carry):
            at = pl.ds(pl.multiple_of(index * tile, tile), tile)
            pre = dot(t_in_t[at, :], all_feats, 1, 1)
            gate = jax.nn.sigmoid(pre)
            hidden_t[at, :] = (pre * gate).astype(BF)
            slope_t[at, :] = (gate * (1.0 + pre * (1.0 - gate))).astype(BF)
            return carry

        lax.fori_loop(0, hidden_width // tile, ahead, 0)
    arrive("term")
    mine_s[...] = jnp.sum(term_r[...].astype(F32), axis=0).astype(BF)
    push("mine")
    arrive("item")
    side = lax.broadcasted_iota(jnp.int32, (rows_table, cands), 0).astype(F32)
    counts_t = jnp.zeros((rows_table, cands), F32)
    for bag in range(bags):
        counts_t = counts_t + jnp.where(rows[bag : bag + 1, :] == side, 1.0, 0.0)
    part_s[...] = dot(counts_t.astype(BF), item_r[...].reshape(cands, width), 1, 0).astype(BF)
    push("part")
    arrive("inter")
    sum_s[...] = jnp.sum(inter_r[...].astype(F32), axis=0).astype(BF)
    push("sum")
    arrive("out")
    g_out[...] = jnp.sum(out_r[...], axis=0)
    arrive("mine")
    if in_place:
        d_users = users_r[...].reshape(all_rows, width)
        d_users_t = d_users.T
        feats_t = all_feats.T

        def behind(index, carry):
            at = pl.ds(pl.multiple_of(index * tile, tile), tile)
            tower_b[at, :] = dot(hidden_t[at, :], d_users, 1, 0)
            d_hidden = dot(t_out[at, :], d_users_t, 1, 0)
            d_pre = (d_hidden * slope_t[at, :].astype(F32)).astype(BF)
            tower_a[:, at] = dot(feats_t, d_pre, 1, 1)
            return carry

        lax.fori_loop(0, hidden_width // tile, behind, 0)
    else:
        tower_a[...] = feat_r[...]
        tower_b[...] = users_r[...]
    arrive("part")
    g_table[...] = jnp.sum(part_r[...].astype(F32), axis=0)
    arrive("sum")
    g_inter[...] = sum_r[...].astype(F32)
    for name in links:
        pltpu.make_async_copy(others(name), others(name), send_sem.at[links[name][0]]).wait()


def body(
    user_feats, tower_in, tower_out, table, inter_weight, out_weight, ids, live, req_of, labels
):
    groups = lax.axis_size("grp")
    shards = lax.axis_size("tbl")
    total = groups * shards
    rows_table, width = table.shape
    slots = ids.shape[3]
    cands = shards * slots
    rows_user, feats = user_feats.shape
    hidden_width = tower_out.shape[0]
    units = inter_weight.shape[1]
    rows_all = total * rows_user
    tile = math.gcd(hidden_width, 512)
    in_place = rows_all <= 512

    slot_index = jnp.arange(slots, dtype=jnp.int32)
    mask = (slot_index[None, :] < live[0][:, None]).reshape(1, cands)
    rows = jnp.concatenate(
        [
            jnp.swapaxes(ids[0], 0, 1).reshape(-1, cands).astype(F32),
            req_of[0].reshape(1, cands).astype(F32),
            mask.astype(F32),
            labels[0].reshape(1, cands),
            jnp.zeros((1, cands), F32),
        ]
    )
    struct = jax.ShapeDtypeStruct
    outs = [
        struct((cands, 1), F32),
        struct((total, width // total, units), F32),
        struct((1, units), F32),
        struct((rows_table, width), F32),
    ]
    if in_place:
        outs += [struct(tower_in.shape, F32), struct(tower_out.shape, F32)]
    else:
        outs += [struct((total, rows_user, feats), BF), struct((total, rows_user, width), BF)]
    blocks = (shards, slots, width)
    terms = (shards, rows_user, width)
    inter = (total, width // total, units)
    buffers = [
        (blocks, BF), (blocks, BF), ((total, rows_user, feats), BF),
        (blocks, BF), (blocks, BF), (terms, BF), (terms, BF),
        (inter, BF), (inter, BF), ((1, units), F32), ((total, 1, units), F32),
        ((rows_user, width), BF), ((total, rows_user, width), BF),
        ((rows_table, width), BF), ((groups, rows_table, width), BF),
        (inter[1:], BF), (inter, BF),
    ]
    if in_place:
        buffers += [
            ((hidden_width, feats), BF),
            ((hidden_width, rows_all), BF),
            ((hidden_width, rows_all), BF),
        ]
    vmem = pl.BlockSpec(memory_space=pltpu.VMEM)
    score, inter_total, out_total, grad_table, first, second = pl.pallas_call(
        functools.partial(step_kernel, groups, shards, slots, ids.shape[2], tile, in_place),
        out_shape=outs,
        in_specs=[vmem] * 8,
        out_specs=[vmem] * 6,
        scratch_shapes=[pltpu.VMEM(shape, kind) for shape, kind in buffers]
        + [pltpu.SemaphoreType.DMA((10,))] * 3,
        compiler_params=pltpu.CompilerParams(
            collective_id=0, has_side_effects=True, vmem_limit_bytes=60 * 1024 * 1024
        ),
        name="ranking_step",
    )(
        user_feats, tower_in, tower_out, table, inter_weight,
        out_weight.reshape(1, units), rows.T, rows,
    )

    def tower_grads(part_feats, part_users):
        pre = dot(part_feats, tower_in, 1, 0)
        hidden = jax.nn.silu(pre).astype(BF)
        grad_out_part = dot(hidden, part_users, 0, 0)
        d_pre = (dot(part_users, tower_out, 1, 1) * silu_slope(pre)).astype(BF)
        return dot(part_feats, d_pre, 0, 0), grad_out_part

    if not in_place:
        all_feats = first.reshape(rows_all, feats)
        d_users = second.reshape(rows_all, width)
        chunk = math.gcd(rows_all, 512)

        def step(index, sums):
            one, two = tower_grads(
                lax.dynamic_slice_in_dim(all_feats, index * chunk, chunk, 0),
                lax.dynamic_slice_in_dim(d_users, index * chunk, chunk, 0),
            )
            return sums[0] + one, sums[1] + two

        first, second = lax.fori_loop(
            0,
            rows_all // chunk,
            step,
            (jnp.zeros(tower_in.shape, F32), jnp.zeros(tower_out.shape, F32)),
        )
    return (
        score.reshape(1, shards, slots),
        first,
        second,
        inter_total.reshape(width, units),
        out_total.reshape(units),
        grad_table,
    )


def solution(mesh):
    placed = (
        P(("grp", "tbl"), None),
        P(),
        P(),
        P("tbl", None),
        P(),
        P(),
        P(("grp", "tbl"), None, None, None),
        P(("grp", "tbl"), None),
        P(("grp", "tbl"), None, None),
        P(("grp", "tbl"), None, None),
    )
    return jax.shard_map(
        body,
        mesh=mesh,
        in_specs=placed,
        out_specs=(P(("grp", "tbl"), None, None), P(), P(), P(), P(), P("tbl", None)),
        check_vma=False,
    )
```

```python
import functools
import math

import jax
import jax.numpy as jnp
from jax import lax
from jax.experimental import pallas as pl
from jax.experimental.pallas import tpu as pltpu
from jax.sharding import PartitionSpec as P

BF = jnp.bfloat16
F32 = jnp.float32
MESH = pl.DeviceIdType.MESH


def silu_slope(value):
    sig = jax.nn.sigmoid(value)
    return sig * (1.0 + value * (1.0 - sig))


def dot(a, b, ca, cb):
    return lax.dot_general(a, b, (((ca,), (cb,)), ((), ())), preferred_element_type=F32)


def step_kernel(groups, shards, slots, bags, tile, in_place, *refs):
    refs = list(refs)
    take = lambda n: [refs.pop(0) for _ in range(n)]
    feats, t_in, t_out, table, weight, out_w, ids, live, req_of, labels = take(10)
    scores, g_inter, g_out, g_table, tower_a, tower_b = take(6)
    pool_s, pool_r, feat_r, item_s, item_r, term_s, term_r = take(7)
    inter_s, inter_r, out_s, out_r, mine_s, users_r, part_s, part_r, sum_s, sum_r = take(10)
    if in_place:
        t_in_t, hidden_t, slope_t = take(3)
    send_sem, recv_sem, own_sem = take(3)
    total = groups * shards
    my_grp = lax.axis_index("grp")
    my_tbl = lax.axis_index("tbl")
    me = my_grp * shards + my_tbl
    rows_table, width = table.shape
    hidden_width = t_out.shape[0]
    units = weight.shape[1]
    cands = shards * slots
    rows_user = feats.shape[0]
    group_rows = shards * rows_user
    sizes = {"all": total, "tbl": shards, "grp": groups, "far": total - shards + 1}
    places = {"all": me, "tbl": my_tbl, "grp": my_grp}
    links = {
        "pool": (0, "tbl", pool_s, pool_r, True),
        "near": (1, "tbl", feats, feat_r, False),
        "far": (2, "far", feats, feat_r, False),
        "item": (3, "tbl", item_s, item_r, True),
        "term": (4, "tbl", term_s, term_r, True),
        "inter": (5, "all", inter_s, inter_r, True),
        "out": (6, "all", out_s, out_r, False),
        "mine": (7, "all", mine_s, users_r, False),
        "part": (8, "grp", part_s, part_r, False),
        "sum": (9, "all", sum_s, sum_r, False),
    }

    def spot(name):
        return me if name in ("near", "far") else places[links[name][1]]

    def origin(name, where):
        _, _, source, _, scatter = links[name]
        return source.at[where] if scatter else source

    def own(name):
        sem, _, _, target, _ = links[name]
        here = spot(name)
        return pltpu.make_async_copy(origin(name, here), target.at[here], own_sem.at[sem])

    def push(*names):
        scope = links[names[0]][1]
        for name in names:
            if name != "far":
                own(name).start()

        def one(step, carry):
            if scope == "all":
                there = lax.rem(me + step, total)
                device = (there // shards, there % shards)
            elif scope == "tbl":
                there = lax.rem(my_tbl + step, shards)
                device = (my_grp, there)
            elif scope == "grp":
                there = lax.rem(my_grp + step, groups)
                device = (there, my_tbl)
            else:
                there = lax.rem((my_grp + 1) * shards + step - 1, total)
                device = (there // shards, there % shards)
            for name in names:
                sem, _, _, target, _ = links[name]
                pltpu.make_async_remote_copy(
                    src_ref=origin(name, there),
                    dst_ref=target.at[spot(name)],
                    send_sem=send_sem.at[sem],
                    recv_sem=recv_sem.at[sem],
                    device_id=device,
                    device_id_type=MESH,
                ).start()
            return carry

        lax.fori_loop(1, sizes[scope], one, 0)

    def others(name):
        _, scope, _, target, _ = links[name]
        return target.at[pl.ds(0, sizes[scope] - 1)]

    def arrive(name):
        if name != "far":
            own(name).wait()
        pltpu.make_async_copy(others(name), others(name), recv_sem.at[links[name][0]]).wait()

    barrier = pltpu.get_barrier_semaphore()

    def greet(step, carry):
        peer = lax.rem(me + step, total)
        pl.semaphore_signal(
            barrier, inc=1, device_id=(peer // shards, peer % shards), device_id_type=MESH
        )
        return carry

    lax.fori_loop(1, total, greet, 0)

    slot = lax.broadcasted_iota(jnp.int32, (shards, slots), 1)
    live_at = jnp.broadcast_to(live[...], (8, shards)).astype(F32).T[:, 0:1]
    mask = jnp.where(slot.astype(F32) < live_at, 1.0, 0.0)
    flat = lambda grid: jnp.concatenate([grid[d : d + 1] for d in range(shards)], axis=1)
    rows = jnp.concatenate(
        [
            jnp.concatenate([ids[0, d].astype(F32) for d in range(shards)], axis=1),
            flat(req_of[0].astype(F32)),
            flat(mask),
            flat(labels[0]),
            jnp.zeros((-(bags + 3) % 8, cands), F32),
        ],
        axis=0,
    )
    cols = rows.T
    lane = lax.broadcasted_iota(jnp.int32, (cands, rows_table), 1).astype(F32)
    counts = jnp.zeros((cands, rows_table), F32)
    for bag in range(bags):
        counts = counts + jnp.where(cols[:, bag : bag + 1] == lane, 1.0, 0.0)
    pooled = dot(counts.astype(BF), table[...], 1, 0)
    pool_s[...] = pooled.reshape(shards, slots, width).astype(BF)
    pl.semaphore_wait(barrier, total - 1)
    push("near", "pool")
    push("far")
    if in_place:

        def flip(index, carry):
            at = pl.ds(pl.multiple_of(index * tile, tile), tile)
            t_in_t[at, :] = t_in[:, at].T
            return carry

        lax.fori_loop(0, hidden_width // tile, flip, 0)

    arrive("near")
    group_feats = feat_r[pl.ds(my_grp * shards, shards)].reshape(group_rows, -1)

    def forward(index, acc):
        at = pl.ds(pl.multiple_of(index * tile, tile), tile)
        pre = dot(group_feats, t_in[:, at], 1, 0)
        hidden = (pre * jax.nn.sigmoid(pre)).astype(BF)
        return acc + dot(hidden, t_out[at, :], 1, 0)

    users = lax.fori_loop(
        0, hidden_width // tile, forward, jnp.zeros((group_rows, width), F32)
    ).astype(BF)
    lane = lax.broadcasted_iota(jnp.int32, (cands, group_rows), 1).astype(F32)
    picks = jnp.where(cols[:, bags : bags + 1] == lane, 1.0, 0.0).astype(BF)
    chosen = dot(picks, users, 1, 0)
    arrive("pool")
    items = pool_r[...].reshape(cands, width).astype(F32)
    cross = (items * chosen).astype(BF)
    inner = dot(cross, weight[...], 1, 0)
    sig = jax.nn.sigmoid(inner)
    act = inner * sig
    score = jnp.sum(act * out_w[...], axis=1, keepdims=True)
    wide = jnp.broadcast_to(score, (cands, 128)).T
    for d in range(shards):
        scores[0, d : d + 1, :] = wide[0:1, d * slots : (d + 1) * slots]
    factor = 1.0 / math.sqrt(groups * shards * shards * slots)
    grad = cols[:, bags + 1 : bags + 2] * (jax.nn.sigmoid(score) - cols[:, bags + 2 : bags + 3]) * factor
    slope = sig * (1.0 + inner * (1.0 - sig))
    dinner = (grad * out_w[...] * slope).astype(BF)
    dcross = dot(dinner, weight[...], 1, 1)
    item_s[...] = (dcross * chosen).reshape(shards, slots, width).astype(BF)
    side = lax.broadcasted_iota(jnp.int32, (group_rows, cands), 0).astype(F32)
    picks_t = jnp.where(rows[bags : bags + 1, :] == side, 1.0, 0.0).astype(BF)
    terms = dot(picks_t, (dcross * items).astype(BF), 1, 0)
    term_s[...] = terms.reshape(shards, rows_user, width).astype(BF)
    push("term", "item")
    out_s[...] = jnp.sum(grad * act, axis=0, keepdims=True)
    inter = dot(cross, dinner, 0, 0)
    inter_s[...] = inter.reshape(total, width // total, units).astype(BF)
    push("inter", "out")
    arrive("far")
    all_rows = total * rows_user
    if in_place:
        all_feats = feat_r[...].reshape(all_rows, -1)

        def ahead(index, carry):
            at = pl.ds(pl.multiple_of(index * tile, tile), tile)
            pre = dot(t_in_t[at, :], all_feats, 1, 1)
            gate = jax.nn.sigmoid(pre)
            hidden_t[at, :] = (pre * gate).astype(BF)
            slope_t[at, :] = (gate * (1.0 + pre * (1.0 - gate))).astype(BF)
            return carry

        lax.fori_loop(0, hidden_width // tile, ahead, 0)
    arrive("term")
    mine_s[...] = jnp.sum(term_r[...].astype(F32), axis=0).astype(BF)
    push("mine")
    arrive("item")
    side = lax.broadcasted_iota(jnp.int32, (rows_table, cands), 0).astype(F32)
    counts_t = jnp.zeros((rows_table, cands), F32)
    for bag in range(bags):
        counts_t = counts_t + jnp.where(rows[bag : bag + 1, :] == side, 1.0, 0.0)
    part_s[...] = dot(counts_t.astype(BF), item_r[...].reshape(cands, width), 1, 0).astype(BF)
    push("part")
    arrive("inter")
    sum_s[...] = jnp.sum(inter_r[...].astype(F32), axis=0).astype(BF)
    push("sum")
    arrive("out")
    g_out[...] = jnp.sum(out_r[...], axis=0)
    arrive("mine")
    if in_place:
        d_users = users_r[...].reshape(all_rows, width)
        d_users_t = d_users.T
        feats_t = all_feats.T

        def behind(index, carry):
            at = pl.ds(pl.multiple_of(index * tile, tile), tile)
            tower_b[at, :] = dot(hidden_t[at, :], d_users, 1, 0).astype(BF)
            d_hidden = dot(t_out[at, :], d_users_t, 1, 0)
            d_pre = (d_hidden * slope_t[at, :].astype(F32)).astype(BF)
            tower_a[:, at] = dot(feats_t, d_pre, 1, 1).astype(BF)
            return carry

        lax.fori_loop(0, hidden_width // tile, behind, 0)
    else:
        tower_a[...] = feat_r[...]
        tower_b[...] = users_r[...]
    arrive("part")
    g_table[...] = jnp.sum(part_r[...].astype(F32), axis=0)
    arrive("sum")
    g_inter[...] = sum_r[...].astype(F32)
    for name in links:
        pltpu.make_async_copy(others(name), others(name), send_sem.at[links[name][0]]).wait()


def body(
    user_feats, tower_in, tower_out, table, inter_weight, out_weight, ids, live, req_of, labels
):
    groups = lax.axis_size("grp")
    shards = lax.axis_size("tbl")
    total = groups * shards
    rows_table, width = table.shape
    slots = ids.shape[3]
    cands = shards * slots
    rows_user, feats = user_feats.shape
    hidden_width = tower_out.shape[0]
    units = inter_weight.shape[1]
    rows_all = total * rows_user
    tile = math.gcd(hidden_width, 512)
    in_place = rows_all <= 512

    struct = jax.ShapeDtypeStruct
    outs = [
        struct((1, shards, slots), F32),
        struct((total, width // total, units), F32),
        struct((1, units), F32),
        struct((rows_table, width), F32),
    ]
    if in_place:
        outs += [struct(tower_in.shape, BF), struct(tower_out.shape, BF)]
    else:
        outs += [struct((total, rows_user, feats), BF), struct((total, rows_user, width), BF)]
    blocks = (shards, slots, width)
    terms = (shards, rows_user, width)
    inter = (total, width // total, units)
    buffers = [
        (blocks, BF), (blocks, BF), ((total, rows_user, feats), BF),
        (blocks, BF), (blocks, BF), (terms, BF), (terms, BF),
        (inter, BF), (inter, BF), ((1, units), F32), ((total, 1, units), F32),
        ((rows_user, width), BF), ((total, rows_user, width), BF),
        ((rows_table, width), BF), ((groups, rows_table, width), BF),
        (inter[1:], BF), (inter, BF),
    ]
    if in_place:
        buffers += [
            ((hidden_width, feats), BF),
            ((hidden_width, rows_all), BF),
            ((hidden_width, rows_all), BF),
        ]
    vmem = pl.BlockSpec(memory_space=pltpu.VMEM)
    score, inter_total, out_total, grad_table, first, second = pl.pallas_call(
        functools.partial(step_kernel, groups, shards, slots, ids.shape[2], tile, in_place),
        out_shape=outs,
        in_specs=[vmem] * 10,
        out_specs=[vmem] * 6,
        scratch_shapes=[pltpu.VMEM(shape, kind) for shape, kind in buffers]
        + [pltpu.SemaphoreType.DMA((10,))] * 3,
        compiler_params=pltpu.CompilerParams(
            collective_id=0, has_side_effects=True, vmem_limit_bytes=60 * 1024 * 1024
        ),
        name="ranking_step",
    )(
        user_feats, tower_in, tower_out, table, inter_weight,
        out_weight.reshape(1, units), ids, live, req_of, labels,
    )

    def tower_grads(part_feats, part_users):
        pre = dot(part_feats, tower_in, 1, 0)
        hidden = jax.nn.silu(pre).astype(BF)
        grad_out_part = dot(hidden, part_users, 0, 0)
        d_pre = (dot(part_users, tower_out, 1, 1) * silu_slope(pre)).astype(BF)
        return dot(part_feats, d_pre, 0, 0), grad_out_part

    if not in_place:
        all_feats = first.reshape(rows_all, feats)
        d_users = second.reshape(rows_all, width)
        chunk = math.gcd(rows_all, 512)

        def step(index, sums):
            one, two = tower_grads(
                lax.dynamic_slice_in_dim(all_feats, index * chunk, chunk, 0),
                lax.dynamic_slice_in_dim(d_users, index * chunk, chunk, 0),
            )
            return sums[0] + one, sums[1] + two

        first, second = lax.fori_loop(
            0,
            rows_all // chunk,
            step,
            (jnp.zeros(tower_in.shape, F32), jnp.zeros(tower_out.shape, F32)),
        )
    return (
        score,
        first.astype(F32),
        second.astype(F32),
        inter_total.reshape(width, units),
        out_total.reshape(units),
        grad_table,
    )


def solution(mesh):
    placed = (
        P(("grp", "tbl"), None),
        P(),
        P(),
        P("tbl", None),
        P(),
        P(),
        P(("grp", "tbl"), None, None, None),
        P(("grp", "tbl"), None),
        P(("grp", "tbl"), None, None),
        P(("grp", "tbl"), None, None),
    )
    return jax.shard_map(
        body,
        mesh=mesh,
        in_specs=placed,
        out_specs=(P(("grp", "tbl"), None, None), P(), P(), P(), P(), P("tbl", None)),
        check_vma=False,
    )
```

```python
import functools
import math

import jax
import jax.numpy as jnp
from jax import lax
from jax.experimental import pallas as pl
from jax.experimental.pallas import tpu as pltpu
from jax.sharding import PartitionSpec as P

BF = jnp.bfloat16
F32 = jnp.float32
MESH = pl.DeviceIdType.MESH


def silu_slope(value):
    sig = jax.nn.sigmoid(value)
    return sig * (1.0 + value * (1.0 - sig))


def dot(a, b, ca, cb):
    return lax.dot_general(a, b, (((ca,), (cb,)), ((), ())), preferred_element_type=F32)


def step_kernel(groups, shards, slots, bags, tile, in_place, *refs):
    refs = list(refs)
    take = lambda n: [refs.pop(0) for _ in range(n)]
    feats, t_in, t_out, table, weight, out_w, ids, live, req_of, labels = take(10)
    scores, g_inter, g_out, g_table, tower_a, tower_b = take(6)
    pool_s, pool_r, feat_r, item_s, item_r, term_s, term_r = take(7)
    half_s, half_r = take(2)
    inter_s, inter_r, out_s, out_r, mine_s, users_r, part_s, part_r, sum_s, sum_r = take(10)
    if in_place:
        t_in_t, hidden_t, slope_t = take(3)
    send_sem, recv_sem, own_sem = take(3)
    total = groups * shards
    my_grp = lax.axis_index("grp")
    my_tbl = lax.axis_index("tbl")
    me = my_grp * shards + my_tbl
    half = total // 2
    core = my_grp % 2
    chip = (my_grp // 2) * shards + my_tbl
    slot_of_me = core * half + chip
    rows_table, width = table.shape
    hidden_width = t_out.shape[0]
    units = weight.shape[1]
    cands = shards * slots
    rows_user = feats.shape[0]
    group_rows = shards * rows_user
    sizes = {"all": total, "tbl": shards, "grp": groups, "far": total - shards + 1, "chip": half, "pair": 2}
    places = {"all": me, "tbl": my_tbl, "grp": my_grp, "chip": chip, "pair": core}
    links = {
        "pool": (0, "tbl", pool_s, pool_r, True),
        "near": (1, "tbl", feats, feat_r, False),
        "far": (2, "far", feats, feat_r, False),
        "item": (3, "tbl", item_s, item_r, True),
        "term": (4, "tbl", term_s, term_r, True),
        "halves": (10, "pair", half_s, half_r, True),
        "inter": (5, "chip", inter_s, inter_r, True),
        "out": (6, "all", out_s, out_r, False),
        "mine": (7, "chip", mine_s, users_r.at[core], False),
        "twin": (11, "pair", users_r.at[core], users_r, False),
        "part": (8, "grp", part_s, part_r, False),
        "sum": (9, "chip", sum_s, sum_r.at[core], False),
        "join": (12, "pair", sum_r.at[core], sum_r, False),
    }

    alone = ("far", "twin", "join")

    def spot(name):
        return slot_of_me if name in ("near", "far") else places[links[name][1]]

    def origin(name, where):
        _, _, source, _, scatter = links[name]
        return source.at[where] if scatter else source

    def own(name):
        sem, _, _, target, _ = links[name]
        here = spot(name)
        return pltpu.make_async_copy(origin(name, here), target.at[here], own_sem.at[sem])

    def push(*names):
        scope = links[names[0]][1]
        for name in names:
            if name not in alone:
                own(name).start()

        def one(step, carry):
            if scope == "all":
                there = lax.rem(me + step, total)
                device = (there // shards, there % shards)
            elif scope == "tbl":
                there = lax.rem(my_tbl + step, shards)
                device = (my_grp, there)
            elif scope == "chip":
                there = lax.rem(chip + step, half)
                device = ((there // shards) * 2 + core, there % shards)
            elif scope == "pair":
                there = 1 - core
                device = (my_grp + 1 - 2 * core, my_tbl)
            elif scope == "grp":
                there = lax.rem(my_grp + step, groups)
                device = (there, my_tbl)
            else:
                there = lax.rem((my_grp + 1) * shards + step - 1, total)
                device = (there // shards, there % shards)
            for name in names:
                sem, _, _, target, _ = links[name]
                pltpu.make_async_remote_copy(
                    src_ref=origin(name, there),
                    dst_ref=target.at[spot(name)],
                    send_sem=send_sem.at[sem],
                    recv_sem=recv_sem.at[sem],
                    device_id=device,
                    device_id_type=MESH,
                ).start()
            return carry

        lax.fori_loop(1, sizes[scope], one, 0)

    def others(name):
        _, scope, _, target, _ = links[name]
        return target.at[pl.ds(0, sizes[scope] - 1)]

    def arrive(name):
        if name not in alone:
            own(name).wait()
        pltpu.make_async_copy(others(name), others(name), recv_sem.at[links[name][0]]).wait()

    barrier = pltpu.get_barrier_semaphore()

    def greet(step, carry):
        peer = lax.rem(me + step, total)
        pl.semaphore_signal(
            barrier, inc=1, device_id=(peer // shards, peer % shards), device_id_type=MESH
        )
        return carry

    lax.fori_loop(1, total, greet, 0)

    slot = lax.broadcasted_iota(jnp.int32, (shards, slots), 1)
    live_at = jnp.broadcast_to(live[...], (8, shards)).astype(F32).T[:, 0:1]
    mask = jnp.where(slot.astype(F32) < live_at, 1.0, 0.0)
    flat = lambda grid: jnp.concatenate([grid[d : d + 1] for d in range(shards)], axis=1)
    rows = jnp.concatenate(
        [
            jnp.concatenate([ids[0, d].astype(F32) for d in range(shards)], axis=1),
            flat(req_of[0].astype(F32)),
            flat(mask),
            flat(labels[0]),
            jnp.zeros((-(bags + 3) % 8, cands), F32),
        ],
        axis=0,
    )
    cols = rows.T
    lane = lax.broadcasted_iota(jnp.int32, (cands, rows_table), 1).astype(F32)
    counts = jnp.zeros((cands, rows_table), F32)
    for bag in range(bags):
        counts = counts + jnp.where(cols[:, bag : bag + 1] == lane, 1.0, 0.0)
    pooled = dot(counts.astype(BF), table[...], 1, 0)
    pool_s[...] = pooled.reshape(shards, slots, width).astype(BF)
    pl.semaphore_wait(barrier, total - 1)
    push("near", "pool")
    push("far")
    if in_place:

        def flip(index, carry):
            at = pl.ds(pl.multiple_of(index * tile, tile), tile)
            t_in_t[at, :] = t_in[:, at].T
            return carry

        lax.fori_loop(0, hidden_width // tile, flip, 0)

    arrive("near")
    group_feats = feat_r[pl.ds(core * half + (my_grp // 2) * shards, shards)].reshape(group_rows, -1)

    def forward(index, acc):
        at = pl.ds(pl.multiple_of(index * tile, tile), tile)
        pre = dot(group_feats, t_in[:, at], 1, 0)
        hidden = (pre * jax.nn.sigmoid(pre)).astype(BF)
        return acc + dot(hidden, t_out[at, :], 1, 0)

    users = lax.fori_loop(
        0, hidden_width // tile, forward, jnp.zeros((group_rows, width), F32)
    ).astype(BF)
    lane = lax.broadcasted_iota(jnp.int32, (cands, group_rows), 1).astype(F32)
    picks = jnp.where(cols[:, bags : bags + 1] == lane, 1.0, 0.0).astype(BF)
    chosen = dot(picks, users, 1, 0)
    arrive("pool")
    items = pool_r[...].reshape(cands, width).astype(F32)
    cross = (items * chosen).astype(BF)
    inner = dot(cross, weight[...], 1, 0)
    sig = jax.nn.sigmoid(inner)
    act = inner * sig
    score = jnp.sum(act * out_w[...], axis=1, keepdims=True)
    wide = jnp.broadcast_to(score, (cands, 128)).T
    for d in range(shards):
        scores[0, d : d + 1, :] = wide[0:1, d * slots : (d + 1) * slots]
    factor = 1.0 / math.sqrt(groups * shards * shards * slots)
    grad = cols[:, bags + 1 : bags + 2] * (jax.nn.sigmoid(score) - cols[:, bags + 2 : bags + 3]) * factor
    slope = sig * (1.0 + inner * (1.0 - sig))
    dinner = (grad * out_w[...] * slope).astype(BF)
    dcross = dot(dinner, weight[...], 1, 1)
    item_s[...] = (dcross * chosen).reshape(shards, slots, width).astype(BF)
    side = lax.broadcasted_iota(jnp.int32, (group_rows, cands), 0).astype(F32)
    picks_t = jnp.where(rows[bags : bags + 1, :] == side, 1.0, 0.0).astype(BF)
    terms = dot(picks_t, (dcross * items).astype(BF), 1, 0)
    term_s[...] = terms.reshape(shards, rows_user, width).astype(BF)
    push("term", "item")
    out_s[...] = jnp.sum(grad * act, axis=0, keepdims=True)
    inter = dot(cross, dinner, 0, 0)
    half_s[...] = inter.reshape(2, width // 2, units).astype(BF)
    push("halves")
    push("out")
    arrive("far")
    all_rows = total * rows_user
    if in_place:
        all_feats = feat_r[...].reshape(all_rows, -1)

        def ahead(index, carry):
            at = pl.ds(pl.multiple_of(index * tile, tile), tile)
            pre = dot(t_in_t[at, :], all_feats, 1, 1)
            gate = jax.nn.sigmoid(pre)
            hidden_t[at, :] = (pre * gate).astype(BF)
            slope_t[at, :] = (gate * (1.0 + pre * (1.0 - gate))).astype(BF)
            return carry

        lax.fori_loop(0, hidden_width // tile, ahead, 0)
    arrive("term")
    mine_s[...] = jnp.sum(term_r[...].astype(F32), axis=0).astype(BF)
    push("mine")
    arrive("halves")
    paired = jnp.sum(half_r[...].astype(F32), axis=0)
    inter_s[...] = paired.reshape(half, width // total, units).astype(BF)
    push("inter")
    arrive("item")
    side = lax.broadcasted_iota(jnp.int32, (rows_table, cands), 0).astype(F32)
    counts_t = jnp.zeros((rows_table, cands), F32)
    for bag in range(bags):
        counts_t = counts_t + jnp.where(rows[bag : bag + 1, :] == side, 1.0, 0.0)
    part_s[...] = dot(counts_t.astype(BF), item_r[...].reshape(cands, width), 1, 0).astype(BF)
    push("part")
    arrive("mine")
    push("twin")
    arrive("inter")
    sum_s[...] = jnp.sum(inter_r[...].astype(F32), axis=0).astype(BF)
    push("sum")
    arrive("out")
    g_out[...] = jnp.sum(out_r[...], axis=0)
    arrive("twin")
    if in_place:
        d_users = users_r[...].reshape(all_rows, width)
        d_users_t = d_users.T
        feats_t = all_feats.T

        def behind(index, carry):
            at = pl.ds(pl.multiple_of(index * tile, tile), tile)
            tower_b[at, :] = dot(hidden_t[at, :], d_users, 1, 0).astype(BF)
            d_hidden = dot(t_out[at, :], d_users_t, 1, 0)
            d_pre = (d_hidden * slope_t[at, :].astype(F32)).astype(BF)
            tower_a[:, at] = dot(feats_t, d_pre, 1, 1).astype(BF)
            return carry

        middle = hidden_width // tile // 2
        lax.fori_loop(0, middle, behind, 0)
        arrive("sum")
        push("join")
        lax.fori_loop(middle, hidden_width // tile, behind, 0)
    else:
        arrive("sum")
        push("join")
        tower_a[...] = feat_r[...]
        tower_b[...] = users_r[...].reshape(tower_b.shape)
    arrive("part")
    g_table[...] = jnp.sum(part_r[...].astype(F32), axis=0)
    arrive("join")
    g_inter[...] = sum_r[...].reshape(g_inter.shape).astype(F32)
    for name in links:
        pltpu.make_async_copy(others(name), others(name), send_sem.at[links[name][0]]).wait()


def body(
    user_feats, tower_in, tower_out, table, inter_weight, out_weight, ids, live, req_of, labels
):
    groups = lax.axis_size("grp")
    shards = lax.axis_size("tbl")
    total = groups * shards
    rows_table, width = table.shape
    slots = ids.shape[3]
    cands = shards * slots
    rows_user, feats = user_feats.shape
    hidden_width = tower_out.shape[0]
    units = inter_weight.shape[1]
    rows_all = total * rows_user
    tile = math.gcd(hidden_width, 512)
    in_place = rows_all <= 512

    struct = jax.ShapeDtypeStruct
    outs = [
        struct((1, shards, slots), F32),
        struct((total, width // total, units), F32),
        struct((1, units), F32),
        struct((rows_table, width), F32),
    ]
    if in_place:
        outs += [struct(tower_in.shape, BF), struct(tower_out.shape, BF)]
    else:
        outs += [struct((total, rows_user, feats), BF), struct((total, rows_user, width), BF)]
    blocks = (shards, slots, width)
    terms = (shards, rows_user, width)
    inter = (total // 2, width // total, units)
    halves = (2, width // 2, units)
    twins = (2, total // 2, rows_user, width)
    buffers = [
        (blocks, BF), (blocks, BF), ((total, rows_user, feats), BF),
        (blocks, BF), (blocks, BF), (terms, BF), (terms, BF),
        (halves, BF), (halves, BF), (inter, BF), (inter, BF), ((1, units), F32), ((total, 1, units), F32),
        ((rows_user, width), BF), (twins, BF),
        ((rows_table, width), BF), ((groups, rows_table, width), BF),
        (inter[1:], BF), ((2,) + inter, BF),
    ]
    if in_place:
        buffers += [
            ((hidden_width, feats), BF),
            ((hidden_width, rows_all), BF),
            ((hidden_width, rows_all), BF),
        ]
    vmem = pl.BlockSpec(memory_space=pltpu.VMEM)
    score, inter_total, out_total, grad_table, first, second = pl.pallas_call(
        functools.partial(step_kernel, groups, shards, slots, ids.shape[2], tile, in_place),
        out_shape=outs,
        in_specs=[vmem] * 10,
        out_specs=[vmem] * 6,
        scratch_shapes=[pltpu.VMEM(shape, kind) for shape, kind in buffers]
        + [pltpu.SemaphoreType.DMA((13,))] * 3,
        compiler_params=pltpu.CompilerParams(
            collective_id=0, has_side_effects=True, vmem_limit_bytes=60 * 1024 * 1024
        ),
        name="ranking_step",
    )(
        user_feats, tower_in, tower_out, table, inter_weight,
        out_weight.reshape(1, units), ids, live, req_of, labels,
    )

    def tower_grads(part_feats, part_users):
        pre = dot(part_feats, tower_in, 1, 0)
        hidden = jax.nn.silu(pre).astype(BF)
        grad_out_part = dot(hidden, part_users, 0, 0)
        d_pre = (dot(part_users, tower_out, 1, 1) * silu_slope(pre)).astype(BF)
        return dot(part_feats, d_pre, 0, 0), grad_out_part

    if not in_place:
        all_feats = first.reshape(rows_all, feats)
        d_users = second.reshape(rows_all, width)
        chunk = math.gcd(rows_all, 512)

        def step(index, sums):
            one, two = tower_grads(
                lax.dynamic_slice_in_dim(all_feats, index * chunk, chunk, 0),
                lax.dynamic_slice_in_dim(d_users, index * chunk, chunk, 0),
            )
            return sums[0] + one, sums[1] + two

        first, second = lax.fori_loop(
            0,
            rows_all // chunk,
            step,
            (jnp.zeros(tower_in.shape, F32), jnp.zeros(tower_out.shape, F32)),
        )
    return (
        score,
        first.astype(F32),
        second.astype(F32),
        inter_total.reshape(width, units),
        out_total.reshape(units),
        grad_table,
    )


def solution(mesh):
    placed = (
        P(("grp", "tbl"), None),
        P(),
        P(),
        P("tbl", None),
        P(),
        P(),
        P(("grp", "tbl"), None, None, None),
        P(("grp", "tbl"), None),
        P(("grp", "tbl"), None, None),
        P(("grp", "tbl"), None, None),
    )
    return jax.shard_map(
        body,
        mesh=mesh,
        in_specs=placed,
        out_specs=(P(("grp", "tbl"), None, None), P(), P(), P(), P(), P("tbl", None)),
        check_vma=False,
    )
```
